32 devices in a mesh: parts: 2 (over x), group: 16 (over z, y, core).
Axes of the slice: x: 2, y: 2, z: 4, core: 2. Of those that a mesh axis runs over, the one named last changes fastest.
Arguments:
- solve_cols: bfloat16 [64, 512, 512], P(('parts', 'group')), parts along dimension 0
- region_groups: int32 [32, 4], P('group'), may hold values from 0 to 15, as said below
Outputs:
- schur: float32 [32, 7, 128, 128], P(('parts', 'group')), parts along dimension 0
The draws below stay inside these ranges and needn't reach their ends.
There are 2 independent parts, one for each index of `parts`. The reference program is written for one: setup_inputs(seed, part) draws one part's arguments, and reference() takes and returns one part's arrays. A program takes and returns all parts, laid end to end along the dimension named above; an argument that names none is the same for every part. Nothing has to cross between parts.
Inputs may be any that keep to these rules, and one draw needn't show every extreme that they name: `region_groups`: the 4 groups of a region are 4 consecutive groups modulo 16, in any order. The 2 regions of one device together name 8 consecutive groups modulo 16, each once, so the slots of one device name one group at most 1 times, and exactly 1 times for some group.
All inputs are finite; a program needn't handle non-finite values.
Results may differ from the reference program's by a relative error of at most 0.00048.
Values may be sent and summed in bfloat16 or wider, within the bound.
A program may use at most 128 MiB of HBM per device.

```python
import math
import jax
import jax.numpy as jnp
from jax import lax

GW = 128
SLOTS = 4
COLS = 512
REACH = 3
ROWS = 512
REG_DEV = 2
GROUPS = 16
REGIONS = 32


def draw_solve_cols(key, part):
    key_noise, key_shared, key_gain = jax.random.split(key, 3)
    noise = jax.random.normal(key_noise, (REGIONS, ROWS, SLOTS, GW), jnp.float32)
    shared = jax.random.normal(key_shared, (REGIONS, ROWS, 1, GW), jnp.float32)
    gains = jax.random.uniform(key_gain, (REGIONS, 1, SLOTS, 1), jnp.float32, 0.5, 1.5)
    values = (noise + 0.8 * gains * shared) * (1.0 / math.sqrt(32.0 * ROWS))
    return values.reshape(REGIONS, ROWS, COLS).astype(jnp.bfloat16)


def draw_region_groups(key, part):
    key_hot, key_near, key_far, key_flag, key_perm = jax.random.split(key, 5)
    device_count = REGIONS // REG_DEV
    hot_group = jax.random.randint(key_hot, (), 0, GROUPS)
    near_shift = jax.random.randint(key_near, (device_count,), -(GROUPS // 8), GROUPS // 8 + 1)
    far_base = jax.random.randint(key_far, (device_count,), 0, GROUPS)
    flags = jax.random.randint(key_flag, (device_count,), 0, 2)
    base_group = jnp.where(flags == 1, hot_group + near_shift, far_base) % GROUPS
    starts = base_group[:, None] + SLOTS * jnp.arange(REG_DEV, dtype=jnp.int32)[None, :]
    scores = jax.random.randint(key_perm, (device_count, REG_DEV, SLOTS), 0, 1000) * SLOTS
    scores = scores + jnp.arange(SLOTS, dtype=jnp.int32)[None, None, :]
    slot_order = jnp.argsort(scores, axis=-1).astype(jnp.int32)
    groups = (starts[:, :, None] + slot_order) % GROUPS
    return groups.reshape(REGIONS, SLOTS).astype(jnp.int32)


def setup_inputs(seed: int = 0, part: int = 0) -> dict:
    key_list = jax.random.split(jax.random.key(seed), 3)
    part_splits = jax.random.split(jax.random.fold_in(key_list[2], part), 3)
    solve_cols = draw_solve_cols(jax.random.fold_in(jax.random.fold_in(key_list[2], part), 71), part)
    region_groups = draw_region_groups(jax.random.fold_in(key_list[2], 71), part)
    return dict(solve_cols=solve_cols, region_groups=region_groups)


def reference(solve_cols, region_groups):
    block_width = COLS // SLOTS
    span_count = 2 * REACH + 1

    def add_region(schur_acc, inputs):
        region_cols, region_slots = inputs
        gram_block = jnp.dot(region_cols.T, region_cols, preferred_element_type=jnp.float32).astype(jnp.bfloat16)
        gram_block = lax.optimization_barrier(gram_block).astype(jnp.float32)
        blocks = gram_block.reshape(SLOTS, block_width, SLOTS, block_width).transpose(0, 2, 1, 3)
        blocks = blocks.reshape(SLOTS * SLOTS, block_width, block_width)
        owners = jnp.repeat(region_slots, SLOTS)
        span_index = ((region_slots[None, :] - region_slots[:, None] + REACH) % GROUPS).reshape(-1)
        schur_acc = schur_acc.at[owners, span_index].add(blocks.astype(schur_acc.dtype))
        return schur_acc, None

    initial = jnp.zeros((GROUPS, span_count, block_width, block_width), jnp.float32)
    schur_out, _ = lax.scan(add_region, initial, (solve_cols, region_groups))
    return schur_out
```

```python
import functools

import jax
import jax.numpy as jnp
from jax import lax
from jax.experimental import pallas as pl
from jax.experimental.pallas import tpu as pltpu
from jax.sharding import PartitionSpec as P

META = 16
CODE_MAX = 32767.0


def each(count, body, first=0):
    if count - first <= 8:
        for i in range(first, count):
            body(i)
    else:
        lax.fori_loop(first, count, lambda i, _: (body(i), None)[1], None)


def rem(a, b):
    return lax.rem(a, jnp.int32(b))


def classes(slots):
    return [*range(1, (slots + 1) // 2), *([slots // 2] if slots % 2 == 0 else []), 0]


def encode(values, code, scale):
    top = jnp.max(jnp.abs(values), axis=0, keepdims=True)
    shift = jnp.where(top > 1.0, 2.0**-32, 2.0**32)
    inverse = jnp.where(top > 0.0, CODE_MAX / (top * shift), 0.0)
    scaled = (values * shift) * inverse
    rounded = jnp.where(scaled >= 0.0, scaled + 0.5, scaled - 0.5)
    code[...] = rounded.astype(jnp.int32).astype(jnp.int16)
    scale[...] = jnp.broadcast_to(top, scale.shape)


def decode(code, scale):
    return (code[...].astype(jnp.int32).astype(jnp.float32) * (1.0 / CODE_MAX)) * scale[0:1, :]


def kernel(
    total_groups,
    groups_hbm,
    cols_hbm,
    out,
    cols,
    gram,
    send,
    recv,
    part,
    code,
    scale,
    code_in,
    scale_in,
    turn,
    turn_scale,
    turn_in,
    turn_scale_in,
    send_sem,
    recv_sem,
    out_sem,
    in_sem,
    turn_sem,
    turn_in_sem,
    cols_sem,
    table,
    groups,
    groups_sem,
):
    groups_copy = pltpu.make_async_copy(groups_hbm, groups, groups_sem)
    groups_copy.start()
    regions, slots = groups.shape
    width = out.shape[-1]
    units = regions * slots
    reach = slots - 1
    me = lax.axis_index("group")
    home = lax.div(me, units)
    residue = rem(me, units)
    partner = rem(me + units, total_groups)
    order = classes(slots)

    def across(step):
        if units & (units - 1):
            return rem(residue + step, units)
        there, digit = residue, 1
        while digit < units:
            flip = rem(lax.div(jnp.int32(step), jnp.int32(digit)), 2)
            there += digit * flip * (1 - 2 * rem(lax.div(residue, jnp.int32(digit)), 2))
            digit *= 2
        return there

    def peer(step):
        return home * units + across(step)

    def at_offset(k):
        return rem(me + total_groups + k, total_groups)

    def owns_half(group):
        i = rem(group, slots)
        low = i < slots // 2
        return (low & (rem(i, 2) == 0)) | (~low & (rem(i + slots // 2, 2) == 1))

    def if_owner(near, group, body, negate=False):
        if 2 * near == slots:
            owner = owns_half(group)
            pl.when(~owner if negate else owner)(body)
        else:
            body()

    barrier = pltpu.get_barrier_semaphore()

    def greet(step):
        pl.semaphore_signal(barrier, inc=1, device_id={"group": peer(step)})

    each(units, greet, 1)
    pl.semaphore_signal(barrier, inc=1, device_id={"group": partner})

    def fetch(r):
        return pltpu.make_async_copy(cols_hbm.at[r], cols.at[r], cols_sem.at[r])

    each(regions, lambda r: fetch(r).start())

    def plan(step):
        want = across(step)

        def found(unit, best):
            there = groups[lax.div(jnp.int32(unit), jnp.int32(slots)), rem(jnp.int32(unit), slots)]
            return jnp.where(rem(there, units) == want, unit, best)

        unit = jnp.int32(0)
        if units <= 8:
            for u in range(1, units):
                unit = found(u, unit)
        else:
            unit = lax.fori_loop(1, units, found, unit)
        r = lax.div(unit, jnp.int32(slots))
        group = groups[r, rem(unit, slots)]
        others = [groups[r, t] for t in range(slots)]
        place = jnp.int32(-1)
        for o in others:
            place += jnp.where(rem(group - o + total_groups, total_groups) <= reach, 1, 0)
        mark = (lax.div(group, jnp.int32(units)) * slots + place).astype(jnp.float32)
        box = recv if isinstance(step, int) and step == 0 else send
        box[step, 0:META, :] = jnp.full((META, width), mark, jnp.float32).astype(box.dtype)
        for c, near in enumerate(order):
            slot = jnp.int32(0)
            for t in range(1, slots):
                slot = jnp.where(rem(others[t], slots) == rem(want + near, slots), t, slot)
            table[step, c] = unit * slots + slot

    groups_copy.wait()
    each(units, plan, 1)
    plan(0)

    def gram_of(r):
        fetch(r).wait()
        full = lax.dot_general(
            cols[r], cols[r], (((0,), (0,)), ((), ())), preferred_element_type=jnp.float32
        ).astype(jnp.bfloat16)
        for s in range(slots):
            for t in range(slots):
                gram[(r * slots + s) * slots + t] = full[
                    s * width : (s + 1) * width, t * width : (t + 1) * width
                ]

    each(regions, gram_of)

    def stage(step, c):
        box = recv if isinstance(step, int) and step == 0 else send
        box[step, META + c * width : META + (c + 1) * width, :] = gram[table[step, c]]

    def rows_of(c):
        return pl.ds(0, META + width) if c == 0 else pl.ds(META + c * width, width)

    def unit_copy(step, c):
        return pltpu.make_async_remote_copy(
            src_ref=send.at[step, rows_of(c), :],
            dst_ref=recv.at[step, rows_of(c), :],
            send_sem=send_sem.at[step, c],
            recv_sem=recv_sem.at[step, c],
            device_id={"group": peer(step)},
        )

    def each_unit_copy(c, act):
        def one(step):
            if_owner(order[c], across(step), lambda: act(unit_copy(step, c)))

        if units <= 8:
            for step in sorted(range(1, units), key=lambda e: (e == 1, e.bit_count(), -e)):
                one(step)
        else:
            each(units, one, 1)

    for c in range(len(order)):
        each(units, lambda step: stage(step, c), 1)
        if c == 0:
            pl.semaphore_wait(barrier, units)
        each_unit_copy(c, lambda copy: copy.start())
    for c in range(len(order)):
        stage(0, c)

    def spans_of(c):
        return [0] if order[c] == 0 else [order[c], order[c] - slots]

    def pair(c, boxes, sems, span, device):
        return [
            pltpu.make_async_remote_copy(
                src_ref=src.at[span],
                dst_ref=dst.at[span],
                send_sem=sems[0].at[c, i],
                recv_sem=sems[1].at[c, i],
                device_id={"group": device},
            )
            for i, (src, dst) in enumerate(boxes)
        ]

    def sum_copies(c):
        span = pl.ds(2 * c, len(spans_of(c)))
        boxes = ((code, code_in), (scale, scale_in))
        return pair(c, boxes, (out_sem, in_sem), span, partner)

    def turn_copies(c, j):
        boxes = ((turn, turn_in), (turn_scale, turn_scale_in))
        at = 2 * c + j
        return pair(at, boxes, (turn_sem, turn_in_sem), at, at_offset(spans_of(c)[j]))

    home_mark = (home * slots).astype(jnp.float32)
    away_mark = (rem(home + 1, 2) * slots).astype(jnp.float32)
    tile = min(width, 32)

    def gather_class(c):
        near, spans = order[c], spans_of(c)
        each(units, lambda step: unit_copy(step, c).wait_recv(), 1)

        def add_tile(i):
            at = i * tile

            def add_unit(step, sums):
                mark = jnp.broadcast_to(recv[step, 0:1, :].astype(jnp.float32), (tile, width))
                block = recv[step, pl.ds(META + c * width + at, tile), :].astype(jnp.float32)
                picked = []
                for base in (home_mark, away_mark):
                    ahead = mark - base
                    if near == 0:
                        picked.append((ahead >= 0.0) & (ahead < float(slots)))
                    else:
                        picked.append((ahead >= 0.0) & (ahead < float(slots - near)))
                        picked.append((ahead >= float(slots - near)) & (ahead < float(slots)))
                return tuple(s + jnp.where(p, block, 0.0) for s, p in zip(sums, picked))

            sums = tuple(jnp.zeros((tile, width), jnp.float32) for _ in range(2 * len(spans)))
            if units <= 8:
                for step in range(units):
                    sums = add_unit(step, sums)
            else:
                sums = lax.fori_loop(0, units, add_unit, sums)
            for j, span in enumerate(spans):
                out[span + reach, pl.ds(at, tile), :] = sums[j]
                part[2 * c + j, pl.ds(at, tile), :] = sums[len(spans) + j]

        each(width // tile, add_tile)
        for j in range(len(spans)):
            encode(part[2 * c + j], code.at[2 * c + j], scale.at[2 * c + j])
        for copy in sum_copies(c):
            copy.start()

    def finish_class(c):
        for copy in sum_copies(c):
            copy.wait_recv()
        for j, span in enumerate(spans_of(c)):
            at = 2 * c + j
            total = out[span + reach] + decode(code_in.at[at], scale_in.at[at])
            out[span + reach] = total
            if span:
                encode(total.T, turn.at[at], turn_scale.at[at])
                for copy in turn_copies(c, j):
                    copy.start()

    def place_turned(c):
        for j, span in enumerate(spans_of(c)):
            for copy in turn_copies(c, j):
                copy.wait_recv()
            out[reach - span] = decode(turn_in.at[2 * c + j], turn_scale_in.at[2 * c + j])

    def drain(c):
        for copy in sum_copies(c):
            copy.wait_send()
        if order[c]:
            for j in range(2):
                for copy in turn_copies(c, j):
                    copy.wait_send()

    last = len(order) - 1
    for c in range(last + 1):
        if_owner(order[c], me, functools.partial(gather_class, c))
        if c:
            if_owner(order[c - 1], me, functools.partial(finish_class, c - 1))
    for c in range(last):
        if_owner(order[c], me, functools.partial(place_turned, c), negate=True)
    finish_class(last)

    for c in range(last + 1):
        each_unit_copy(c, lambda copy: copy.wait_send())
        if_owner(order[c], me, functools.partial(drain, c))


def shards(solve_cols, region_groups):
    regions, slots = region_groups.shape
    width = solve_cols.shape[2] // slots
    total_groups = lax.axis_size("group")
    units = regions * slots
    assert total_groups == 2 * units
    spans = 2 * slots - 1
    count = len(classes(slots))
    sent = 2 * count - 1
    box = pltpu.VMEM((units, META + count * width, width), jnp.bfloat16)
    coded = [pltpu.VMEM((sent, width, width), jnp.int16), pltpu.VMEM((sent, 8, width), jnp.float32)]
    vmem = pl.BlockSpec(memory_space=pltpu.VMEM)
    sums = pl.pallas_call(
        functools.partial(kernel, total_groups),
        out_shape=pltpu.VMEM((spans, width, width), jnp.float32),
        in_specs=[pl.BlockSpec(memory_space=pl.ANY), pl.BlockSpec(memory_space=pl.ANY)],
        out_specs=vmem,
        scratch_shapes=[
            pltpu.VMEM(solve_cols.shape, solve_cols.dtype),
            pltpu.VMEM((units * slots, width, width), jnp.bfloat16),
            box,
            box,
            pltpu.VMEM((sent, width, width), jnp.float32),
            *(coded * 4),
            pltpu.SemaphoreType.DMA((units, count)),
            pltpu.SemaphoreType.DMA((units, count)),
            pltpu.SemaphoreType.DMA((count, 2)),
            pltpu.SemaphoreType.DMA((count, 2)),
            pltpu.SemaphoreType.DMA((sent, 2)),
            pltpu.SemaphoreType.DMA((sent, 2)),
            pltpu.SemaphoreType.DMA((regions,)),
            pltpu.SMEM((units, count), jnp.int32),
            pltpu.SMEM(region_groups.shape, jnp.int32),
            pltpu.SemaphoreType.DMA(()),
        ],
        compiler_params=pltpu.CompilerParams(
            collective_id=0, has_side_effects=True, vmem_limit_bytes=60 * 1024 * 1024
        ),
    )(region_groups, solve_cols)
    return sums[None]


def solution(mesh):
    return jax.shard_map(
        shards,
        mesh=mesh,
        in_specs=(P(("parts", "group"), None, None), P("group", None)),
        out_specs=P(("parts", "group"), None, None, None),
        check_vma=False,
    )
```

```python
import functools

import jax
import jax.numpy as jnp
from jax import lax
from jax.experimental import pallas as pl
from jax.experimental.pallas import tpu as pltpu
from jax.sharding import PartitionSpec as P

META = 16
CODE_MAX = 32767.0
CUTS = {}


def each(count, body, first=0):
    if count - first <= 8:
        for i in range(first, count):
            body(i)
    else:
        lax.fori_loop(first, count, lambda i, _: (body(i), None)[1], None)


def rem(a, b):
    return lax.rem(a, jnp.int32(b))


def classes(slots):
    return [*range(1, (slots + 1) // 2), *([slots // 2] if slots % 2 == 0 else []), 0]


def encode(values, code, scale):
    top = jnp.max(jnp.abs(values), axis=0, keepdims=True)
    shift = jnp.where(top > 1.0, 2.0**-32, 2.0**32)
    inverse = jnp.where(top > 0.0, CODE_MAX / (top * shift), 0.0)
    scaled = (values * shift) * inverse
    rounded = jnp.where(scaled >= 0.0, scaled + 0.5, scaled - 0.5)
    code[...] = rounded.astype(jnp.int32).astype(jnp.int16)
    scale[...] = jnp.broadcast_to(top, scale.shape)


def decode(code, scale):
    return (code[...].astype(jnp.int32).astype(jnp.float32) * (1.0 / CODE_MAX)) * scale[0:1, :]


def pieces_of(slots, width, cuts):
    pieces, start = [], META
    for c, near in enumerate(classes(slots)):
        count = cuts.get(near, 1)
        rows = width // count if near else width // 2
        for i in range(count):
            pieces.append((c, near, i * rows, rows, start))
            start += rows
    return pieces, start


def lanes_rows(rows, width):
    shape = (rows, width)
    return lax.broadcasted_iota(jnp.int32, shape, 1), lax.broadcasted_iota(jnp.int32, shape, 0)


def fold(square):
    width = square.shape[1]
    half = width // 2
    lane, row = lanes_rows(half, width)
    low = pltpu.roll(square[half:], half, 1)
    folded = jnp.where((lane >= half) | (lane <= row), square[:half], low)
    diagonal = jnp.sum(jnp.where(lane == row, low, 0.0), axis=0, keepdims=True)
    return folded, diagonal


def unfold(folded, diagonal):
    half, width = folded.shape
    lane, row = lanes_rows(half, width)
    turned = jnp.concatenate([folded, jnp.zeros_like(folded)], axis=0).T
    top = jnp.where((lane >= half) | (lane <= row), folded, turned[:half])
    corner = jnp.where(lane > row, folded, jnp.where(lane < row, turned[:half], diagonal))
    return top, jnp.where(lane < half, turned[half:], pltpu.roll(corner, half, 1))


def steps_of(pieces):
    last = len(pieces) - 1
    steps = [("send", p) for p in range(last)]
    steps += [("own", p) for p in range(last + 1)]
    steps += [("gather", 0), ("send", last)]
    steps += [("gather", p) for p in range(1, last)]
    steps += [("finish", 0), ("gather", last)]
    steps += [("finish", p) for p in range(1, last + 1)]
    return steps + [("place", near) for near in dict.fromkeys(q[1] for q in pieces) if near]


def kernel(
    total_groups,
    groups_hbm,
    cols_hbm,
    out,
    cols,
    gram,
    send,
    recv,
    part,
    folded_sum,
    code,
    scale,
    code_in,
    scale_in,
    turn,
    turn_scale,
    turn_in,
    turn_scale_in,
    send_sem,
    recv_sem,
    out_sem,
    in_sem,
    turn_sem,
    turn_in_sem,
    cols_sem,
    table,
    groups,
    groups_sem,
):
    groups_copy = pltpu.make_async_copy(groups_hbm, groups, groups_sem)
    groups_copy.start()
    regions, slots = groups.shape
    width = out.shape[-1]
    units = regions * slots
    reach = slots - 1
    me = lax.axis_index("group")
    home = lax.div(me, units)
    residue = rem(me, units)
    partner = rem(me + units, total_groups)
    order = classes(slots)
    half = width // 2
    pieces, _ = pieces_of(slots, width, CUTS)

    def across(step):
        if units & (units - 1):
            return rem(residue + step, units)
        there, digit = residue, 1
        while digit < units:
            flip = rem(lax.div(jnp.int32(step), jnp.int32(digit)), 2)
            there += digit * flip * (1 - 2 * rem(lax.div(residue, jnp.int32(digit)), 2))
            digit *= 2
        return there

    def peer(step):
        return home * units + across(step)

    def at_offset(k):
        return rem(me + total_groups + k, total_groups)

    def owns_half(group):
        i = rem(group, slots)
        low = i < slots // 2
        return (low & (rem(i, 2) == 0)) | (~low & (rem(i + slots // 2, 2) == 1))

    def if_owner(near, group, body, negate=False):
        if 2 * near == slots:
            owner = owns_half(group)
            pl.when(~owner if negate else owner)(body)
        else:
            body()

    barrier = pltpu.get_barrier_semaphore()

    def greet(step):
        pl.semaphore_signal(barrier, inc=1, device_id={"group": peer(step)})

    each(units, greet, 1)
    pl.semaphore_signal(barrier, inc=1, device_id={"group": partner})

    def fetch(r):
        return pltpu.make_async_copy(cols_hbm.at[r], cols.at[r], cols_sem.at[r])

    each(regions, lambda r: fetch(r).start())

    def plan(step):
        want = across(step)

        def found(unit, best):
            there = groups[lax.div(jnp.int32(unit), jnp.int32(slots)), rem(jnp.int32(unit), slots)]
            return jnp.where(rem(there, units) == want, unit, best)

        unit = jnp.int32(0)
        if units <= 8:
            for u in range(1, units):
                unit = found(u, unit)
        else:
            unit = lax.fori_loop(1, units, found, unit)
        r = lax.div(unit, jnp.int32(slots))
        group = groups[r, rem(unit, slots)]
        others = [groups[r, t] for t in range(slots)]
        place = jnp.int32(-1)
        for o in others:
            place += jnp.where(rem(group - o + total_groups, total_groups) <= reach, 1, 0)
        mark = (lax.div(group, jnp.int32(units)) * slots + place).astype(jnp.float32)
        box = recv if isinstance(step, int) and step == 0 else send
        box[step, 0:META, :] = jnp.full((META, width), mark, jnp.float32).astype(box.dtype)
        for c, near in enumerate(order):
            slot = jnp.int32(0)
            for t in range(1, slots):
                slot = jnp.where(rem(others[t], slots) == rem(want + near, slots), t, slot)
            table[step, c] = unit * slots + slot

    groups_copy.wait()
    each(units, plan, 1)
    plan(0)

    def gram_of(r):
        fetch(r).wait()
        full = lax.dot_general(
            cols[r], cols[r], (((0,), (0,)), ((), ())), preferred_element_type=jnp.float32
        )
        for s in range(slots):
            for t in range(slots):
                block = full[s * width : (s + 1) * width, t * width : (t + 1) * width]
                at = (r * slots + s) * slots + t
                if s != t:
                    gram[at] = block.astype(jnp.bfloat16)
                else:
                    folded, diagonal = fold(block)
                    gram[at, :half, :] = folded.astype(jnp.bfloat16)
                    gram[at, half : half + META, :] = jnp.broadcast_to(
                        diagonal, (META, width)
                    ).astype(jnp.bfloat16)

    each(regions, gram_of)

    def stage(step, p):
        c, near, at, rows, start = pieces[p]
        box = recv if isinstance(step, int) and step == 0 else send
        box[step, start : start + rows, :] = gram[table[step, c], at : at + rows, :]
        if p == 0:
            diagonal = gram[table[step, len(order) - 1], half : half + META, :].astype(jnp.float32)
            mark = box[step, 0:META, :].astype(jnp.float32)
            _, row = lanes_rows(META, width)
            box[step, 0:META, :] = jnp.where(row < 8, mark, diagonal).astype(box.dtype)

    def unit_copy(step, p):
        c, near, at, rows, start = pieces[p]
        span = pl.ds(0, META + rows) if p == 0 else pl.ds(start, rows)
        return pltpu.make_async_remote_copy(
            src_ref=send.at[step, span, :],
            dst_ref=recv.at[step, span, :],
            send_sem=send_sem.at[step, p],
            recv_sem=recv_sem.at[step, p],
            device_id={"group": peer(step)},
        )

    def each_unit_copy(p, act):
        def one(step):
            if_owner(pieces[p][1], across(step), lambda: act(unit_copy(step, p)))

        if units <= 8:
            for step in sorted(range(1, units), key=lambda e: (e == 1, e.bit_count(), -e)):
                one(step)
        else:
            each(units, one, 1)

    def send_piece(p):
        each_unit_copy(p, lambda copy: copy.start())

    def spans_of(near):
        return [0] if near == 0 else [near, near - slots]

    def pair(at, boxes, sems, device):
        return [
            pltpu.make_async_remote_copy(
                src_ref=src,
                dst_ref=dst,
                send_sem=sems[0].at[at, i],
                recv_sem=sems[1].at[at, i],
                device_id={"group": device},
            )
            for i, (src, dst) in enumerate(boxes)
        ]

    def sum_copies(p):
        c, near, at, rows, _ = pieces[p]
        spans = len(spans_of(near))
        values = pl.ds(2 * c, spans), pl.ds(at, rows if near else half)
        tops = pl.ds(2 * p, 2)
        boxes = ((code.at[*values], code_in.at[*values]), (scale.at[tops], scale_in.at[tops]))
        return pair(p, boxes, (out_sem, in_sem), partner)

    def turn_copies(p, j):
        c, near, at, rows, _ = pieces[p]
        values = 2 * c + j, pl.ds(at, rows)
        boxes = (
            (turn.at[*values], turn_in.at[*values]),
            (turn_scale.at[2 * p + j], turn_scale_in.at[2 * p + j]),
        )
        return pair(2 * p + j, boxes, (turn_sem, turn_in_sem), at_offset(spans_of(near)[j]))

    home_mark = (home * slots).astype(jnp.float32)
    away_mark = (rem(home + 1, 2) * slots).astype(jnp.float32)

    def add_diagonal(p):
        c = pieces[p][0]

        def add_unit(step, sums):
            ahead = recv[step, 0:1, :].astype(jnp.float32)
            row = recv[step, 8:9, :].astype(jnp.float32)
            picked = []
            for base in (home_mark, away_mark):
                picked.append((ahead >= base) & (ahead < base + float(slots)))
            return tuple(s + jnp.where(q, row, 0.0) for s, q in zip(sums, picked))

        sums = tuple(jnp.zeros((1, width), jnp.float32) for _ in range(2))
        if units <= 8:
            for step in range(units):
                sums = add_unit(step, sums)
        else:
            sums = lax.fori_loop(0, units, add_unit, sums)
        folded_sum[half : half + 8, :] = jnp.broadcast_to(sums[0], (8, width))
        scale[2 * p + 1] = sums[1]

    def gather(p):
        c, near, at, rows, start = pieces[p]
        spans = spans_of(near)
        tile = META if rows % 32 else 32
        each(units, lambda step: unit_copy(step, p).wait_recv(), 1)

        def add_tile(i):
            row = i * tile

            def add_unit(step, sums):
                mark = jnp.broadcast_to(recv[step, 0:1, :].astype(jnp.float32), (tile, width))
                block = recv[step, pl.ds(start + row, tile), :].astype(jnp.float32)
                picked = []
                for base in (home_mark, away_mark):
                    ahead = mark - base
                    if near == 0:
                        picked.append((ahead >= 0.0) & (ahead < float(slots)))
                    else:
                        picked.append((ahead >= 0.0) & (ahead < float(slots - near)))
                        picked.append((ahead >= float(slots - near)) & (ahead < float(slots)))
                return tuple(s + jnp.where(q, block, 0.0) for s, q in zip(sums, picked))

            sums = tuple(jnp.zeros((tile, width), jnp.float32) for _ in range(2 * len(spans)))
            if units <= 8:
                for step in range(units):
                    sums = add_unit(step, sums)
            else:
                sums = lax.fori_loop(0, units, add_unit, sums)
            for j, span in enumerate(spans):
                if near:
                    out[span + reach, pl.ds(at + row, tile), :] = sums[j]
                else:
                    folded_sum[pl.ds(row, tile), :] = sums[j]
                part[2 * c + j, pl.ds(at + row, tile), :] = sums[len(spans) + j]

        each(rows // tile, add_tile)
        if not near:
            add_diagonal(p)
        for j in range(len(spans)):
            if near:
                values = pl.ds(at, rows)
                encode(part[2 * c + j, values, :], code.at[2 * c + j, values], scale.at[2 * p + j])
            else:
                encode(part[2 * c, :half, :], code.at[2 * c, :half], scale.at[2 * p])
        for copy in sum_copies(p):
            copy.start()

    def finish(p):
        c, near, at, rows, _ = pieces[p]
        for copy in sum_copies(p):
            copy.wait_recv()
        if not near:
            total = folded_sum[:half, :] + decode(code_in.at[2 * c, :half], scale_in.at[2 * p])
            diagonal = folded_sum[half : half + 1, :] + scale_in[2 * p + 1]
            out[reach, :half, :], out[reach, half:, :] = unfold(total, diagonal)
            return
        for j, span in enumerate(spans_of(near)):
            values = pl.ds(at, rows)
            total = out[span + reach, values, :] + decode(
                code_in.at[2 * c + j, values], scale_in.at[2 * p + j]
            )
            out[span + reach, values, :] = total
            encode(total, turn.at[2 * c + j, values], turn_scale.at[2 * p + j])
            for copy in turn_copies(p, j):
                copy.start()

    def place(near):
        for j, span in enumerate(spans_of(near)):
            rows_in = []
            for p, (c, its_near, at, rows, _) in enumerate(pieces):
                if its_near == near:
                    for copy in turn_copies(p, j):
                        copy.wait_recv()
                    rows_in.append(
                        decode(turn_in.at[2 * c + j, pl.ds(at, rows)], turn_scale_in.at[2 * p + j])
                    )
            block = rows_in[0] if len(rows_in) == 1 else jnp.concatenate(rows_in, axis=0)
            out[reach - span] = block.T

    def drain(p):
        for copy in sum_copies(p):
            copy.wait_send()
        if pieces[p][1]:
            for j in range(2):
                for copy in turn_copies(p, j):
                    copy.wait_send()

    def owned(act, p):
        if_owner(pieces[p][1], me, functools.partial(act, p))

    for act, p in steps_of(pieces):
        if act == "send":
            each(units, lambda step: stage(step, p), 1)
            if p == 0:
                pl.semaphore_wait(barrier, units)
            send_piece(p)
        elif act == "own":
            stage(0, p)
        elif act == "gather":
            owned(gather, p)
        elif act == "finish":
            owned(finish, p)
        else:
            if_owner(p, me, functools.partial(place, p), negate=True)

    for p in range(len(pieces)):
        each_unit_copy(p, lambda copy: copy.wait_send())
        owned(drain, p)


def shards(solve_cols, region_groups):
    regions, slots = region_groups.shape
    width = solve_cols.shape[2] // slots
    total_groups = lax.axis_size("group")
    units = regions * slots
    assert total_groups == 2 * units
    spans = 2 * slots - 1
    count = len(classes(slots))
    sent = 2 * count - 1
    pieces, height = pieces_of(slots, width, CUTS)
    many = len(pieces)
    box = pltpu.VMEM((units, height, width), jnp.bfloat16)
    coded = [pltpu.VMEM((sent, width, width), jnp.int16), pltpu.VMEM((2 * many, 1, width), jnp.float32)]
    vmem = pl.BlockSpec(memory_space=pltpu.VMEM)
    sums = pl.pallas_call(
        functools.partial(kernel, total_groups),
        out_shape=pltpu.VMEM((spans, width, width), jnp.float32),
        in_specs=[pl.BlockSpec(memory_space=pl.ANY), pl.BlockSpec(memory_space=pl.ANY)],
        out_specs=vmem,
        scratch_shapes=[
            pltpu.VMEM(solve_cols.shape, solve_cols.dtype),
            pltpu.VMEM((units * slots, width, width), jnp.bfloat16),
            box,
            box,
            pltpu.VMEM((sent, width, width), jnp.float32),
            pltpu.VMEM((width // 2 + 8, width), jnp.float32),
            *(coded * 4),
            *([pltpu.SemaphoreType.DMA((units, many))] * 2),
            *([pltpu.SemaphoreType.DMA((many, 2))] * 2),
            *([pltpu.SemaphoreType.DMA((2 * many, 2))] * 2),
            pltpu.SemaphoreType.DMA((regions,)),
            pltpu.SMEM((units, count), jnp.int32),
            pltpu.SMEM(region_groups.shape, jnp.int32),
            pltpu.SemaphoreType.DMA(()),
        ],
        compiler_params=pltpu.CompilerParams(
            collective_id=0, has_side_effects=True, vmem_limit_bytes=60 * 1024 * 1024
        ),
    )(region_groups, solve_cols)
    return sums[None]


def solution(mesh):
    return jax.shard_map(
        shards,
        mesh=mesh,
        in_specs=(P(("parts", "group"), None, None), P("group", None)),
        out_specs=P(("parts", "group"), None, None, None),
        check_vma=False,
    )
```
